512 devices in a mesh: seq: 64 (over z, y), head: 8 (over x, core).
Axes of the slice: x: 4, y: 4, z: 16, core: 2. Of those that a mesh axis runs over, the one named last changes fastest.
Arguments:
- query_rows: bfloat16 [16384, 4096], P('seq', 'head'), may hold values from -5.5 to 5.5
- key_rows: bfloat16 [16384, 4096], P('seq', 'head'), may hold values from -5.5 to 5.5
- value_rows: bfloat16 [16384, 4096], P('seq', 'head'), may hold values from -6 to 6
- cluster_ids: int32 [16, 16384, 1], P('head', 'seq'), may hold values from 0 to 255; in each aligned block of 256 rows (0 to 255, 256 to 511, ..., all dimensions but the last counted through in order) at most 2 rows name the same one
Outputs:
- attended: bfloat16 [16384, 4096], P('seq', 'head')
The draws below stay inside these ranges and needn't reach their ends.
Inputs may be any that keep to these rules, and one draw needn't show every extreme that they name: `cluster_ids`: for each routing head, the 256 tokens of one index of seq name any one cluster at most 2 times, and some cluster exactly that often.
All inputs are finite; a program needn't handle non-finite values.
Results may differ from the reference program's by a relative error of at most 0.0045.
Values may be sent and summed in bfloat16 or wider, within the bound.
A program may use at most 64 MiB of HBM per device.

```python
import math
import jax
import jax.numpy as jnp
import numpy as np
from jax import lax

HEADS = 32
HD = 128
CLUSTERS = 256
WINDOW = 1024
TOK_DEV = 256
SRC_CAP = 2
TOKENS = 16384
ROUTE_HEADS = 16
PAIR = 2
CAP = 128
N_SEQ = 64
N_HEAD = 8


def drawn_rows(key, salt_value):
    own_key = jax.random.fold_in(key, salt_value)
    row_shape = (TOKENS, HEADS * HD)
    drawn = jnp.clip(jax.random.normal(own_key, row_shape, jnp.float32), -5.5, 5.5)
    return drawn.astype(jnp.bfloat16)


def draw_query_rows(key, part):
    return drawn_rows(key, 1)


def draw_key_rows(key, part):
    return drawn_rows(key, 2)


def shard_levels(rng, extent, pieces, least, top_value):
    gain, own = 1.0, jax.random.fold_in(rng, 6)
    for dim, parts in pieces:
        steps = jnp.exp(jax.random.uniform(jax.random.fold_in(own, dim), (parts,), jnp.float32, least / len(pieces), top_value / len(pieces)))
        gain = gain * jnp.repeat(steps, extent[dim] // parts).reshape([-1 if axis == dim else 1 for axis in range(len(extent))])
    return gain


def routed_block(rng, own, number, rows, amount, top, bound, skew):
    sequence = jax.random.permutation(rng, amount)
    heavy_load, usual = load_shares(amount, rows * top, bound, skew, True), load_shares(amount, rows * top, bound, skew, False)
    places = jnp.arange(amount)

    def named(tallies, offset_by):
        used = int((tallies > 0).sum())
        fixed = max(1, used // 4)
        moved = fixed + (places - fixed + offset_by * (used - fixed)) % max(1, amount - fixed)
        return jnp.zeros((amount,), jnp.int32).at[sequence[jnp.where(places < fixed, places, moved)]].set(jnp.asarray(tallies, jnp.int32))

    tallies = jnp.where(number % 4 == 0, named(heavy_load, number // 4), named(usual, number - number // 4 - 1))
    mixed = jax.random.permutation(jax.random.fold_in(own, 3), amount)
    source_of, sink = mixed[0:amount // 2 * 2:2], mixed[1:amount // 2 * 2:2]
    margin = jnp.minimum(tallies[source_of] - 1, bound - tallies[sink]) // 2
    margin = jnp.where((source_of == sequence[0]) | (sink == sequence[0]) | (tallies[sink] == 0), 0, jnp.maximum(margin, 0))
    moved = jax.random.randint(jax.random.fold_in(own, 4), (amount // 2,), 0, 1 << 20) % (margin + 1)
    tallies = tallies.at[source_of].add(-moved).at[sink].add(moved)
    items = jnp.searchsorted(jnp.cumsum(tallies), jnp.arange(rows * top), side="right").astype(jnp.int32)
    table = items.reshape(top, rows).T
    table = table[jax.random.permutation(jax.random.fold_in(own, 1), rows)]
    offset_by = jax.random.randint(jax.random.fold_in(own, 2), (rows, 1), 0, top)
    return jnp.take_along_axis(table, (jnp.arange(top)[None, :] + offset_by) % top, axis=1)


def load_shares(count, total, bound, lean, full):
    portions = [(1 << 20) // math.isqrt(rank ** lean) + 1 for rank in range(1, count + 1)]
    largest = bound if full else min(bound, max(-(-total // count), total * portions[0] // sum(portions)))
    least = 1 if total - largest >= count - 1 else 0
    given, rest = [largest] + [least] * (count - 1), total - largest - least * (count - 1)
    while rest > 0:
        free = [i for i in range(1, count) if given[i] < largest] or [i for i in range(1, count) if given[i] < bound]
        whole, budget = sum([portions[i] for i in free]), rest
        for i in free:
            more = min(bound - given[i], max(1, budget * portions[i] // whole), rest)
            given[i] = given[i] + more
            rest = rest - more
    return np.array(given)


def noise(stream_key, shape, scale, reach, shards=(), held_as=jnp.bfloat16):
    loudness = shard_levels(stream_key, shape, shards, -0.22, 0.18) if shards else 1.0
    array = jax.random.normal(stream_key, shape, jnp.float32) * scale * loudness
    return jnp.minimum(jnp.maximum(array, -reach), reach).astype(held_as)


def setup_inputs(seed: int = 0) -> dict:
    key_of = jax.random.split(jax.random.key(seed), 5)
    query_rows = draw_query_rows(jax.random.fold_in(key_of[4], 71), 0)
    key_rows = draw_key_rows(jax.random.fold_in(key_of[4], 71), 0)
    value_rows = noise(key_of[2], (TOKENS, HEADS * HD), 1.0, 6.0, ((0, 64), (1, 8)))
    cluster_ids_keys = jax.random.split(jax.random.fold_in(key_of[3], 1), ROUTE_HEADS * TOKENS // TOK_DEV)
    cluster_ids_turns = jax.random.permutation(jax.random.fold_in(key_of[3], 3), ROUTE_HEADS * TOKENS // TOK_DEV)
    cluster_ids = jax.vmap(lambda own, number: routed_block(jax.random.fold_in(key_of[3], 2), own, number, TOK_DEV, CLUSTERS, 1, SRC_CAP, 2))(cluster_ids_keys, cluster_ids_turns).reshape((ROUTE_HEADS, TOKENS, 1))
    return dict(query_rows=query_rows, key_rows=key_rows, value_rows=value_rows, cluster_ids=cluster_ids)


NEG_FILL = -1e+30

def blend_rows(scores, allowed, value_block):
    scores = jnp.where(allowed, scores, NEG_FILL)
    largest = lax.optimization_barrier(jnp.max(scores, axis=-1, keepdims=True))
    raised = jnp.exp(scores - largest)
    weights = (raised / lax.optimization_barrier(jnp.sum(raised, axis=-1, keepdims=True))).astype(jnp.bfloat16)
    return jnp.dot(weights, value_block, preferred_element_type=jnp.float32).astype(jnp.bfloat16)

def local_head(head, query_rows, key_rows, value_rows):
    scale = 1.0 / math.sqrt(HD)
    block = min(512, TOKENS)
    query_head = lax.dynamic_slice_in_dim(query_rows, head * HD, HD, 1)
    key_head = lax.dynamic_slice_in_dim(key_rows, head * HD, HD, 1)
    value_head = lax.dynamic_slice_in_dim(value_rows, head * HD, HD, 1)
    padding = jnp.zeros((WINDOW, HD), jnp.bfloat16)
    key_padded = jnp.concatenate([padding, key_head], 0)
    value_padded = jnp.concatenate([padding, value_head], 0)

    def one_block(index):
        start = (index * block).astype(jnp.int32)
        query_block = lax.dynamic_slice_in_dim(query_head, start, block, 0)
        key_block = lax.dynamic_slice_in_dim(key_padded, start, block + WINDOW, 0)
        value_block = lax.dynamic_slice_in_dim(value_padded, start, block + WINDOW, 0)
        query_pos = start + jnp.arange(block, dtype=jnp.int32)
        key_pos = start - WINDOW + jnp.arange(block + WINDOW, dtype=jnp.int32)
        allowed = (key_pos[None, :] <= query_pos[:, None]) & (key_pos[None, :] > query_pos[:, None] - WINDOW) & (key_pos[None, :] >= 0)
        scores = jnp.dot(query_block, key_block.T, preferred_element_type=jnp.float32) * scale
        return blend_rows(scores, allowed, value_block)
    return lax.map(one_block, jnp.arange(TOKENS // block, dtype=jnp.int32)).reshape(TOKENS, HD)

def routed_head(route, query_rows, key_rows, value_rows, cluster_ids):
    scale = 1.0 / math.sqrt(HD)
    head = route // PAIR * (2 * PAIR) + PAIR + route % PAIR
    query_head = lax.dynamic_slice_in_dim(query_rows, head * HD, HD, 1)
    key_head = lax.dynamic_slice_in_dim(key_rows, head * HD, HD, 1)
    value_head = lax.dynamic_slice_in_dim(value_rows, head * HD, HD, 1)
    labels = lax.dynamic_index_in_dim(cluster_ids, route, 0, keepdims=False)[:, 0].reshape(N_SEQ, TOK_DEV)
    onehot = (labels[:, :, None] == jnp.arange(CLUSTERS, dtype=jnp.int32)).astype(jnp.int32)
    rank = lax.optimization_barrier(jnp.sum(jnp.cumsum(onehot, axis=1) * onehot, axis=-1)) - 1
    slot = (labels * CAP + jnp.arange(N_SEQ, dtype=jnp.int32)[:, None] * SRC_CAP + rank).reshape(TOKENS).astype(jnp.int32)
    token_of = jnp.full((CLUSTERS * CAP,), -1, jnp.int32).at[slot].set(jnp.arange(TOKENS, dtype=jnp.int32))
    safe_rows = jnp.maximum(token_of, 0)
    query_group = query_head[safe_rows].reshape(CLUSTERS, CAP, HD)
    key_group = key_head[safe_rows].reshape(CLUSTERS, CAP, HD)
    value_group = value_head[safe_rows].reshape(CLUSTERS, CAP, HD)
    positions = token_of.reshape(CLUSTERS, CAP)

    def one_cluster(operands):
        query_block, key_block, value_block, where_at = operands
        allowed = (where_at[None, :] <= where_at[:, None]) & (where_at[None, :] >= 0)
        scores = jnp.dot(query_block, key_block.T, preferred_element_type=jnp.float32) * scale
        return blend_rows(scores, allowed, value_block)
    mixed = lax.map(one_cluster, (query_group, key_group, value_group, positions)).reshape(CLUSTERS * CAP, HD)
    return mixed[slot]

def reference(query_rows, key_rows, value_rows, cluster_ids):
    routes = jnp.arange(ROUTE_HEADS, dtype=jnp.int32)
    local_ids = routes // PAIR * (2 * PAIR) + routes % PAIR

    def run_local(head):
        return local_head(head, query_rows, key_rows, value_rows)

    def run_routed(route):
        return routed_head(route, query_rows, key_rows, value_rows, cluster_ids)
    local_out = lax.map(run_local, local_ids).reshape(N_HEAD, PAIR, TOKENS, HD)
    routed_out = lax.map(run_routed, routes).reshape(N_HEAD, PAIR, TOKENS, HD)
    joined = jnp.stack([local_out, routed_out], 1).reshape(HEADS, TOKENS, HD)
    return joined.transpose(1, 0, 2).reshape(TOKENS, HEADS * HD)
```

```python
import math

import jax
import jax.numpy as jnp
from jax import lax
from jax.experimental import pallas as pl
from jax.experimental.pallas import tpu as pltpu
from jax.sharding import PartitionSpec as P

CLUSTERS = 256
SRC_CAP = 2
SEQ = 64
ROWS_Z = 16
ROWS_Y = 4
TOK = 256
HD = 128
PAIR = 2
SPLIT = PAIR * HD
OWNED = CLUSTERS // SEQ
ROOM = OWNED * SRC_CAP
SLOTS = SEQ * ROOM
SPAN = 4
MASKED = -1e30
EMPTY = 2.0**60
EMPTY_TEST = 2.0**50
NT = (((1,), (1,)), ((), ()))


def dot(a, b, dims=(((1,), (0,)), ((), ()))):
    return lax.dot_general(a, b, dims, preferred_element_type=jnp.float32)


def blend(scores, value_block):
    largest = jnp.max(scores, axis=-1, keepdims=True)
    raised = jnp.exp(scores - largest)
    weights = (raised * (1.0 / jnp.sum(raised, axis=-1, keepdims=True))).astype(jnp.bfloat16)
    return dot(weights, value_block)


def kernel(q_ref, k_ref, v_ref, idc_ref, idr_ref, out_ref,
           send, recv, osend, home, win,
           own_sem, send_sem, recv_sem, osend_sem, home_sem, win_send, win_recv):
    me = lax.axis_index("seq")
    z, y = me // ROWS_Y, me % ROWS_Y
    scale = 1.0 / math.sqrt(HD)

    def each_peer(act):
        def step(i, carry):
            m = (i + 1) // 2
            dz = (8 - m) * (2 * (i % 2) - 1)
            pz = (z + dz + ROWS_Z) % ROWS_Z
            for dy in range(ROWS_Y):
                act(pz * ROWS_Y + (y + dy) % ROWS_Y)
            return carry

        lax.fori_loop(0, ROWS_Z - 1, step, 0)
        for dy in range(1, ROWS_Y):
            act(z * ROWS_Y + (y + dy) % ROWS_Y)

    barrier = pltpu.get_barrier_semaphore()
    each_peer(lambda peer: pl.semaphore_signal(barrier, inc=1, device_id={"seq": peer}))

    own_k = pltpu.make_async_copy(k_ref.at[:, pl.ds(0, SPLIT)], win.at[0, :, pl.ds(0, SPLIT)], own_sem.at[0])
    own_v = pltpu.make_async_copy(v_ref.at[:, pl.ds(0, SPLIT)], win.at[0, :, pl.ds(SPLIT, SPLIT)], own_sem.at[1])
    own_k.start()
    own_v.start()

    earlier = lax.broadcasted_iota(jnp.int32, (TOK, TOK), 0) < lax.broadcasted_iota(jnp.int32, (TOK, TOK), 1)
    later = lax.broadcasted_iota(jnp.int32, (TOK, TOK), 0) > lax.broadcasted_iota(jnp.int32, (TOK, TOK), 1)
    slot_cols = []
    for h in range(PAIR):
        id_col = idc_ref[h]
        id_row = idr_ref[h:h + 1, :]
        same = id_col == id_row
        rank_row = jnp.sum(jnp.where(same & earlier, 1, 0), axis=0, keepdims=True)
        rank_col = jnp.sum(jnp.where(same & later, 1, 0), axis=1, keepdims=True)
        slot_row = id_row * SRC_CAP + rank_row
        slot_cols.append(id_col * SRC_CAP + rank_col)
        pick = jnp.where(lax.broadcasted_iota(jnp.int32, (SLOTS, TOK), 0) == slot_row, 1.0, 0.0)
        blank = (1.0 - jnp.sum(pick, axis=1, keepdims=True)) * EMPTY
        pick = pick.astype(jnp.bfloat16)
        cols = pl.ds(SPLIT + h * HD, HD)
        packed_q = dot(pick, q_ref[:, cols])
        packed_k = dot(pick, k_ref[:, cols])
        packed_v = dot(pick, v_ref[:, cols]) + blank
        for n, packed in enumerate((packed_q, packed_k, packed_v)):
            send[h, :, :, n * HD:(n + 1) * HD] = packed.reshape(SEQ, ROOM, HD).astype(jnp.bfloat16)

    own_k.wait()
    own_v.wait()
    pl.semaphore_wait(barrier, SEQ - 1)

    def push(source, target, from_sem, to_sem):
        def act(peer):
            pltpu.make_async_remote_copy(
                src_ref=source.at[peer], dst_ref=target.at[me],
                send_sem=from_sem, recv_sem=to_sem, device_id={"seq": peer},
            ).start()
        return act

    def arrived(buffer, from_sem, to_sem):
        return pltpu.make_async_remote_copy(
            src_ref=buffer.at[pl.ds(0, SEQ - 1)], dst_ref=buffer.at[pl.ds(0, SEQ - 1)],
            send_sem=from_sem, recv_sem=to_sem, device_id={"seq": (me + 1) % SEQ},
        )

    def own_chunk(source, target, sem):
        return pltpu.make_async_copy(source.at[me], target.at[me], sem)

    for h in range(PAIR):
        each_peer(push(send.at[h], recv.at[h], send_sem.at[h], recv_sem.at[h]))
        own_chunk(send.at[h], recv.at[h], own_sem.at[2 + h]).start()

    def window(src_slot, dst_slot, peer):
        return pltpu.make_async_remote_copy(
            src_ref=win.at[src_slot], dst_ref=win.at[dst_slot],
            send_sem=win_send.at[dst_slot - 1], recv_sem=win_recv.at[dst_slot - 1],
            device_id={"seq": peer},
        )

    ahead = window(0, SPAN, (me + ROWS_Y) % SEQ)
    ahead.start()

    def sideways(dy):
        return window(SPAN * ((y + dy) // ROWS_Y), dy, z * ROWS_Y + (y + dy) % ROWS_Y)

    for dy in range(1, ROWS_Y):
        @pl.when(y + dy < ROWS_Y)
        def _(dy=dy):
            sideways(dy).start()

    def routed(h):
        arrived(recv.at[h], send_sem.at[h], recv_sem.at[h]).wait_recv()
        own_chunk(send.at[h], recv.at[h], own_sem.at[2 + h]).wait()
        q, k, v = (
            recv[h, :, :, n * HD:(n + 1) * HD].astype(jnp.float32).reshape(SLOTS, HD).astype(jnp.bfloat16)
            for n in range(3)
        )
        probe = jnp.where(lax.broadcasted_iota(jnp.int32, (16, HD), 1) == 0, 1.0, 0.0).astype(jnp.bfloat16)
        first = dot(probe, v, NT)[0:1, :]
        absent = jnp.where(first > EMPTY_TEST, MASKED, 0.0)
        block = 128
        for b in range(SLOTS // block):
            lo, hi = b * block, (b + 1) * block
            row = lax.broadcasted_iota(jnp.int32, (block, hi), 0) + lo
            col = lax.broadcasted_iota(jnp.int32, (block, hi), 1)
            allowed = (col <= row) & ((row & (ROOM - SRC_CAP)) == (col & (ROOM - SRC_CAP)))
            scores = dot(q[lo:hi], k[:hi], NT) * scale + absent[:, :hi]
            mixed = blend(jnp.where(allowed, scores, MASKED), v[:hi])
            osend[h, b * 16:(b + 1) * 16] = mixed.reshape(16, ROOM, HD).astype(jnp.bfloat16)
        each_peer(push(osend.at[h], home.at[h], osend_sem.at[h], home_sem.at[h]))
        own_chunk(osend.at[h], home.at[h], own_sem.at[4 + h]).start()

    routed(0)
    ahead.wait_recv()
    for dy in range(1, ROWS_Y):
        @pl.when(y + dy >= ROWS_Y)
        def _(dy=dy):
            sideways(dy).start()
    routed(1)

    for dy in range(1, ROWS_Y):
        sideways(dy).wait_recv()
    width = (SPAN + 1) * TOK
    row = lax.broadcasted_iota(jnp.int32, (TOK, width), 0)
    col = lax.broadcasted_iota(jnp.int32, (TOK, width), 1)
    slot, at = col // TOK, col % TOK
    gap = row - at + slot * TOK
    allowed = (gap >= 0) & (gap < SPAN * TOK) & (slot <= me)
    for h in range(PAIR):
        k = win[:, :, h * HD:(h + 1) * HD].reshape(width, HD)
        v = win[:, :, SPLIT + h * HD:SPLIT + (h + 1) * HD].reshape(width, HD)
        scores = dot(q_ref[:, h * HD:(h + 1) * HD], k, NT) * scale
        mixed = blend(jnp.where(allowed, scores, MASKED), v)
        out_ref[:, h * HD:(h + 1) * HD] = mixed.astype(jnp.bfloat16)

    for h in range(PAIR):
        back = jnp.where(lax.broadcasted_iota(jnp.int32, (TOK, SLOTS), 1) == slot_cols[h], 1.0, 0.0).astype(jnp.bfloat16)
        arrived(home.at[h], osend_sem.at[h], home_sem.at[h]).wait_recv()
        own_chunk(osend.at[h], home.at[h], own_sem.at[4 + h]).wait()
        rows = home[h].astype(jnp.float32).reshape(SLOTS, HD).astype(jnp.bfloat16)
        out_ref[:, SPLIT + h * HD:SPLIT + (h + 1) * HD] = dot(back, rows).astype(jnp.bfloat16)

    for h in range(PAIR):
        arrived(recv.at[h], send_sem.at[h], recv_sem.at[h]).wait_send()
        arrived(home.at[h], osend_sem.at[h], home_sem.at[h]).wait_send()
    ahead.wait_send()
    for dy in range(1, ROWS_Y):
        sideways(dy).wait_send()


def per_device(query_rows, key_rows, value_rows, cluster_ids):
    vmem = pl.BlockSpec(memory_space=pltpu.VMEM)
    return pl.pallas_call(
        kernel,
        out_shape=jax.ShapeDtypeStruct(query_rows.shape, jnp.bfloat16),
        in_specs=[vmem] * 5,
        out_specs=vmem,
        scratch_shapes=[
            pltpu.VMEM((PAIR, SEQ, ROOM, 3 * HD), jnp.bfloat16),
            pltpu.VMEM((PAIR, SEQ, ROOM, 3 * HD), jnp.bfloat16),
            pltpu.VMEM((PAIR, SEQ, ROOM, HD), jnp.bfloat16),
            pltpu.VMEM((PAIR, SEQ, ROOM, HD), jnp.bfloat16),
            pltpu.VMEM((SPAN + 1, TOK, 2 * SPLIT), jnp.bfloat16),
            pltpu.SemaphoreType.DMA((6,)),
            pltpu.SemaphoreType.DMA((PAIR,)),
            pltpu.SemaphoreType.DMA((PAIR,)),
            pltpu.SemaphoreType.DMA((PAIR,)),
            pltpu.SemaphoreType.DMA((PAIR,)),
            pltpu.SemaphoreType.DMA((SPAN,)),
            pltpu.SemaphoreType.DMA((SPAN,)),
        ],
        compiler_params=pltpu.CompilerParams(
            collective_id=0, has_side_effects=True, vmem_limit_bytes=48 * 1024 * 1024
        ),
    )(query_rows, key_rows, value_rows, cluster_ids, cluster_ids[:, :, 0])


def solution(mesh):
    in_specs = (P("seq", "head"), P("seq", "head"), P("seq", "head"), P("head", "seq", None))
    out_specs = P("seq", "head")
    return jax.shard_map(
        per_device, mesh=mesh, in_specs=in_specs, out_specs=out_specs, check_vma=False
    )
```

```python
import math

import jax
import jax.numpy as jnp
from jax import lax
from jax.experimental import pallas as pl
from jax.experimental.pallas import tpu as pltpu
from jax.sharding import PartitionSpec as P

CLUSTERS = 256
SRC_CAP = 2
SEQ = 64
ROWS_Z = 16
ROWS_Y = 4
TOK = 256
HD = 128
PAIR = 2
SPLIT = PAIR * HD
OWNED = CLUSTERS // SEQ
ROOM = OWNED * SRC_CAP
SLOTS = SEQ * ROOM
SPAN = 4
MASKED = -1e30
EMPTY = 2.0**60
EMPTY_TEST = 2.0**50
NT = (((1,), (1,)), ((), ()))


def dot(a, b, dims=(((1,), (0,)), ((), ()))):
    return lax.dot_general(a, b, dims, preferred_element_type=jnp.float32)


def blend(scores, value_block):
    largest = jnp.max(scores, axis=-1, keepdims=True)
    raised = jnp.exp(scores - largest)
    weights = (raised * (1.0 / jnp.sum(raised, axis=-1, keepdims=True))).astype(jnp.bfloat16)
    return dot(weights, value_block)


def kernel(q_hbm, k_hbm, v_hbm, id_hbm, out_ref,
           q_ref, k_ref, v_ref, id_ref, send, recv, osend, home, win, stop,
           load_sem, own_sem, send_sem, recv_sem, osend_sem, home_sem, win_send, win_recv, ready,
           leg_send, leg_recv, hop_send):
    me = lax.axis_index("seq")
    z, y = me // ROWS_Y, me % ROWS_Y
    scale = 1.0 / math.sqrt(HD)

    def at_distance(dz, act, away=True):
        for dy in range(ROWS_Y):
            if away or dy:
                act((z + dz + ROWS_Z) % ROWS_Z * ROWS_Y + (y + dy) % ROWS_Y)

    def each_peer(act, nearer=0):
        def step(i, carry):
            m = (i + 1) // 2
            at_distance((8 - m) * (2 * (i % 2) - 1), act)
            return carry

        lax.fori_loop(nearer, ROWS_Z - 1, step, 0)
        at_distance(0, act, False)

    barrier = pltpu.get_barrier_semaphore()

    def greet(peer):
        pl.semaphore_signal(barrier, inc=1, device_id={"seq": peer})

    for dz in (1, -1, 0):
        at_distance(dz, greet, dz != 0)

    def widen(n):
        for dz in (1 << n, -(1 << n)):
            peer = (z + dz + ROWS_Z) % ROWS_Z * ROWS_Y + y
            pl.semaphore_signal(ready.at[n], inc=1, device_id={"seq": peer})

    loads = [
        pltpu.make_async_copy(source, target, load_sem.at[n])
        for n, (source, target) in enumerate(
            ((id_hbm, id_ref), (q_hbm, q_ref), (k_hbm, k_ref), (v_hbm, v_ref),
             (k_hbm.at[:, pl.ds(0, SPLIT)], win.at[0, :, pl.ds(0, SPLIT)]),
             (v_hbm.at[:, pl.ds(0, SPLIT)], win.at[0, :, pl.ds(SPLIT, SPLIT)]))
        )
    ]
    for load in loads:
        load.start()

    def window(src_slot, dst_slot, peer):
        return pltpu.make_async_remote_copy(
            src_ref=win.at[src_slot], dst_ref=win.at[dst_slot],
            send_sem=win_send.at[dst_slot - 1], recv_sem=win_recv.at[dst_slot - 1],
            device_id={"seq": peer},
        )

    ahead = window(0, SPAN, (me + ROWS_Y) % SEQ)

    def sideways(dy):
        return window(SPAN * ((y + dy) // ROWS_Y), dy, z * ROWS_Y + (y + dy) % ROWS_Y)

    pl.semaphore_wait(barrier, 3 * ROWS_Y - 1)
    widen(0)
    for load in loads:
        load.wait()
    ahead.start()
    for dy in range(1, ROWS_Y):
        @pl.when(y + dy < ROWS_Y)
        def _(dy=dy):
            sideways(dy).start()

    earlier = lax.broadcasted_iota(jnp.int32, (TOK, TOK), 0) < lax.broadcasted_iota(jnp.int32, (TOK, TOK), 1)
    later = lax.broadcasted_iota(jnp.int32, (TOK, TOK), 0) > lax.broadcasted_iota(jnp.int32, (TOK, TOK), 1)
    diagonal = ~(earlier | later)
    slot_cols = []
    for h in range(PAIR):
        id_row = id_ref[h]
        id_col = jnp.sum(jnp.where(diagonal, id_row, 0), axis=1, keepdims=True)
        same = id_col == id_row
        rank_row = jnp.sum(jnp.where(same & earlier, 1, 0), axis=0, keepdims=True)
        rank_col = jnp.sum(jnp.where(same & later, 1, 0), axis=1, keepdims=True)
        slot_row = id_row * SRC_CAP + rank_row
        slot_cols.append(id_col * SRC_CAP + rank_col)
        pick = jnp.where(lax.broadcasted_iota(jnp.int32, (SLOTS, TOK), 0) == slot_row, 1.0, 0.0)
        blank = (1.0 - jnp.sum(pick, axis=1, keepdims=True)) * EMPTY
        pick = pick.astype(jnp.bfloat16)
        cols = pl.ds(SPLIT + h * HD, HD)
        packed_q = dot(pick, q_ref[:, cols])
        packed_k = dot(pick, k_ref[:, cols])
        packed_v = dot(pick, v_ref[:, cols]) + blank
        for n, packed in enumerate((packed_q, packed_k, packed_v)):
            send[h, :, :, n * HD:(n + 1) * HD] = packed.reshape(SEQ, ROOM, HD).astype(jnp.bfloat16)

    def push(source, target, from_sem, to_sem):
        def act(peer):
            pltpu.make_async_remote_copy(
                src_ref=source.at[peer], dst_ref=target.at[me],
                send_sem=from_sem, recv_sem=to_sem, device_id={"seq": peer},
            ).start()
        return act

    def leg(h, dy):
        to_y = (y + dy) % ROWS_Y
        return pltpu.make_async_remote_copy(
            src_ref=send.at[h, (z + 8) % ROWS_Z * ROWS_Y + to_y], dst_ref=stop.at[h, y],
            send_sem=leg_send.at[h], recv_sem=leg_recv.at[h],
            device_id={"seq": (z + 12) % ROWS_Z * ROWS_Y + to_y},
        )

    def legs(h):
        return pltpu.make_async_remote_copy(
            src_ref=stop.at[h], dst_ref=stop.at[h], send_sem=leg_send.at[h], recv_sem=leg_recv.at[h],
            device_id={"seq": (me + 1) % SEQ},
        )

    def onward(h):
        return pltpu.make_async_remote_copy(
            src_ref=stop.at[h], dst_ref=recv.at[h, pl.ds((z + 4) % ROWS_Z * ROWS_Y, ROWS_Y)],
            send_sem=hop_send.at[h], recv_sem=recv_sem.at[h],
            device_id={"seq": (z + 12) % ROWS_Z * ROWS_Y + y},
        )

    def arrived(buffer, from_sem, to_sem):
        return pltpu.make_async_remote_copy(
            src_ref=buffer.at[pl.ds(0, SEQ - 1)], dst_ref=buffer.at[pl.ds(0, SEQ - 1)],
            send_sem=from_sem, recv_sem=to_sem, device_id={"seq": (me + 1) % SEQ},
        )

    def own_chunk(source, target, sem):
        return pltpu.make_async_copy(source.at[me], target.at[me], sem)

    first_push = push(send.at[0], recv.at[0], send_sem.at[0], recv_sem.at[0])
    for dz in (1, -1, 0):
        at_distance(dz, first_push, dz != 0)
    for n, distances in enumerate(((2,), (4, 3), (7, 6, 5))):
        pl.semaphore_wait(ready.at[n], 2)
        if n < 2:
            widen(n + 1)
        if n == 2:
            for dy in range(ROWS_Y):
                leg(0, dy).start()
        for d in distances:
            at_distance(d, first_push)
            at_distance(-d, first_push)
    for dy in range(ROWS_Y):
        leg(1, dy).start()
    each_peer(push(send.at[1], recv.at[1], send_sem.at[1], recv_sem.at[1]), 1)
    for h in range(PAIR):
        own_chunk(send.at[h], recv.at[h], own_sem.at[h]).start()

    ahead.wait_recv()
    for dy in range(1, ROWS_Y):
        @pl.when(y + dy >= ROWS_Y)
        def _(dy=dy):
            sideways(dy).start()

    for h in range(PAIR):
        legs(h).wait_recv()
        onward(h).start()

    def routed(h):
        arrived(recv.at[h], send_sem.at[h], recv_sem.at[h]).wait_recv()
        own_chunk(send.at[h], recv.at[h], own_sem.at[h]).wait()
        q, k, v = (
            recv[h, :, :, n * HD:(n + 1) * HD].astype(jnp.float32).reshape(SLOTS, HD).astype(jnp.bfloat16)
            for n in range(3)
        )
        probe = jnp.where(lax.broadcasted_iota(jnp.int32, (16, HD), 1) == 0, 1.0, 0.0).astype(jnp.bfloat16)
        first = dot(probe, v, NT)[0:1, :]
        absent = jnp.where(first > EMPTY_TEST, MASKED, 0.0)
        block = 128
        for b in range(SLOTS // block):
            lo, hi = b * block, (b + 1) * block
            row = lax.broadcasted_iota(jnp.int32, (block, hi), 0) + lo
            col = lax.broadcasted_iota(jnp.int32, (block, hi), 1)
            allowed = (col <= row) & ((row & (ROOM - SRC_CAP)) == (col & (ROOM - SRC_CAP)))
            scores = dot(q[lo:hi], k[:hi], NT) * scale + absent[:, :hi]
            mixed = blend(jnp.where(allowed, scores, MASKED), v[:hi])
            osend[h, b * 16:(b + 1) * 16] = mixed.reshape(16, ROOM, HD).astype(jnp.bfloat16)
        each_peer(push(osend.at[h], home.at[h], osend_sem.at[h], home_sem.at[h]))
        own_chunk(osend.at[h], home.at[h], own_sem.at[2 + h]).start()

    routed(0)
    routed(1)

    for dy in range(1, ROWS_Y):
        sideways(dy).wait_recv()
    width = (SPAN + 1) * TOK
    row = lax.broadcasted_iota(jnp.int32, (TOK, width), 0)
    col = lax.broadcasted_iota(jnp.int32, (TOK, width), 1)
    slot, at = col // TOK, col % TOK
    gap = row - at + slot * TOK
    allowed = (gap >= 0) & (gap < SPAN * TOK) & (slot <= me)
    for h in range(PAIR):
        k = win[:, :, h * HD:(h + 1) * HD].reshape(width, HD)
        v = win[:, :, SPLIT + h * HD:SPLIT + (h + 1) * HD].reshape(width, HD)
        scores = dot(q_ref[:, h * HD:(h + 1) * HD], k, NT) * scale
        mixed = blend(jnp.where(allowed, scores, MASKED), v)
        out_ref[:, h * HD:(h + 1) * HD] = mixed.astype(jnp.bfloat16)

    for h in range(PAIR):
        back = jnp.where(lax.broadcasted_iota(jnp.int32, (TOK, SLOTS), 1) == slot_cols[h], 1.0, 0.0).astype(jnp.bfloat16)
        arrived(home.at[h], osend_sem.at[h], home_sem.at[h]).wait_recv()
        own_chunk(osend.at[h], home.at[h], own_sem.at[2 + h]).wait()
        rows = home[h].astype(jnp.float32).reshape(SLOTS, HD).astype(jnp.bfloat16)
        out_ref[:, SPLIT + h * HD:SPLIT + (h + 1) * HD] = dot(back, rows).astype(jnp.bfloat16)

    for h in range(PAIR):
        sent = send.at[h, pl.ds(0, SEQ - 1 - ROWS_Y)]
        pltpu.make_async_remote_copy(
            src_ref=sent, dst_ref=sent, send_sem=send_sem.at[h], recv_sem=recv_sem.at[h],
            device_id={"seq": (me + 1) % SEQ},
        ).wait_send()
        legs(h).wait_send()
        onward(h).wait_send()
        arrived(home.at[h], osend_sem.at[h], home_sem.at[h]).wait_send()
    ahead.wait_send()
    for dy in range(1, ROWS_Y):
        sideways(dy).wait_send()


def per_device(query_rows, key_rows, value_rows, cluster_ids):
    vmem = pl.BlockSpec(memory_space=pltpu.VMEM)
    return pl.pallas_call(
        kernel,
        out_shape=jax.ShapeDtypeStruct(query_rows.shape, jnp.bfloat16),
        in_specs=[pl.BlockSpec(memory_space=pltpu.HBM)] * 4,
        out_specs=vmem,
        scratch_shapes=[
            pltpu.VMEM((TOK, 2 * SPLIT), jnp.bfloat16),
            pltpu.VMEM((TOK, 2 * SPLIT), jnp.bfloat16),
            pltpu.VMEM((TOK, 2 * SPLIT), jnp.bfloat16),
            pltpu.VMEM((PAIR, 1, TOK), jnp.int32),
            pltpu.VMEM((PAIR, SEQ, ROOM, 3 * HD), jnp.bfloat16),
            pltpu.VMEM((PAIR, SEQ, ROOM, 3 * HD), jnp.bfloat16),
            pltpu.VMEM((PAIR, SEQ, ROOM, HD), jnp.bfloat16),
            pltpu.VMEM((PAIR, SEQ, ROOM, HD), jnp.bfloat16),
            pltpu.VMEM((SPAN + 1, TOK, 2 * SPLIT), jnp.bfloat16),
            pltpu.VMEM((PAIR, ROWS_Y, ROOM, 3 * HD), jnp.bfloat16),
            pltpu.SemaphoreType.DMA((6,)),
            pltpu.SemaphoreType.DMA((4,)),
            pltpu.SemaphoreType.DMA((PAIR,)),
            pltpu.SemaphoreType.DMA((PAIR,)),
            pltpu.SemaphoreType.DMA((PAIR,)),
            pltpu.SemaphoreType.DMA((PAIR,)),
            pltpu.SemaphoreType.DMA((SPAN,)),
            pltpu.SemaphoreType.DMA((SPAN,)),
            pltpu.SemaphoreType.REGULAR((3,)),
            pltpu.SemaphoreType.DMA((PAIR,)),
            pltpu.SemaphoreType.DMA((PAIR,)),
            pltpu.SemaphoreType.DMA((PAIR,)),
        ],
        compiler_params=pltpu.CompilerParams(
            collective_id=0, has_side_effects=True, vmem_limit_bytes=67043328
        ),
    )(query_rows, key_rows, value_rows, cluster_ids.transpose(0, 2, 1))


def solution(mesh):
    in_specs = (P("seq", "head"), P("seq", "head"), P("seq", "head"), P("head", "seq", None))
    out_specs = P("seq", "head")
    return jax.shard_map(
        per_device, mesh=mesh, in_specs=in_specs, out_specs=out_specs, check_vma=False
    )
```

```python
import math

import jax
import jax.numpy as jnp
from jax import lax
from jax.experimental import pallas as pl
from jax.experimental.pallas import tpu as pltpu
from jax.sharding import PartitionSpec as P

CLUSTERS = 256
SRC_CAP = 2
SEQ = 64
ROWS_Z = 16
ROWS_Y = 4
TOK = 256
HD = 128
PAIR = 2
SPLIT = PAIR * HD
OWNED = CLUSTERS // SEQ
ROOM = OWNED * SRC_CAP
SLOTS = SEQ * ROOM
SPAN = 4
MASKED = -1e30
EMPTY = 2.0**60
EMPTY_TEST = 2.0**50
NT = (((1,), (1,)), ((), ()))


def dot(a, b, dims=(((1,), (0,)), ((), ()))):
    return lax.dot_general(a, b, dims, preferred_element_type=jnp.float32)


def blend(scores, value_block):
    largest = jnp.max(scores, axis=-1, keepdims=True)
    raised = jnp.exp(scores - largest)
    weights = (raised * (1.0 / jnp.sum(raised, axis=-1, keepdims=True))).astype(jnp.bfloat16)
    return dot(weights, value_block)


def kernel(q_hbm, k_hbm, v_hbm, id_hbm, out_ref,
           q_ref, k_ref, v_ref, id_ref, send, recv, osend, home, win, stop,
           load_sem, own_sem, send_sem, recv_sem, osend_sem, home_sem, win_send, win_recv, ready,
           leg_send, leg_recv, hop_send):
    me = lax.axis_index("seq")
    z, y = me // ROWS_Y, me % ROWS_Y
    scale = 1.0 / math.sqrt(HD)

    def at_distance(dz, act, away=True):
        for dy in range(ROWS_Y):
            if away or dy:
                act((z + dz + ROWS_Z) % ROWS_Z * ROWS_Y + (y + dy) % ROWS_Y)

    def each_peer(act, nearer=0):
        def step(i, carry):
            m = (i + 1) // 2
            at_distance((8 - m) * (2 * (i % 2) - 1), act)
            return carry

        lax.fori_loop(nearer, ROWS_Z - 1, step, 0)
        at_distance(0, act, False)

    barrier = pltpu.get_barrier_semaphore()

    def greet(peer):
        pl.semaphore_signal(barrier, inc=1, device_id={"seq": peer})

    for dz in (1, -1, 0):
        at_distance(dz, greet, dz != 0)

    def widen(n):
        for dz in (1 << n, -(1 << n)):
            peer = (z + dz + ROWS_Z) % ROWS_Z * ROWS_Y + y
            pl.semaphore_signal(ready.at[n], inc=1, device_id={"seq": peer})

    loads = [
        pltpu.make_async_copy(source, target, load_sem.at[n])
        for n, (source, target) in enumerate(
            ((id_hbm, id_ref), (q_hbm, q_ref), (k_hbm, k_ref), (v_hbm, v_ref),
             (k_hbm.at[:, pl.ds(0, SPLIT)], win.at[0, :, pl.ds(0, SPLIT)]),
             (v_hbm.at[:, pl.ds(0, SPLIT)], win.at[0, :, pl.ds(SPLIT, SPLIT)]))
        )
    ]
    for load in loads:
        load.start()

    def window(src_slot, dst_slot, peer):
        return pltpu.make_async_remote_copy(
            src_ref=win.at[src_slot], dst_ref=win.at[dst_slot],
            send_sem=win_send.at[dst_slot - 1], recv_sem=win_recv.at[dst_slot - 1],
            device_id={"seq": peer},
        )

    ahead = window(0, SPAN, (me + ROWS_Y) % SEQ)

    def sideways(dy):
        return window(SPAN * ((y + dy) // ROWS_Y), dy, z * ROWS_Y + (y + dy) % ROWS_Y)

    pl.semaphore_wait(barrier, 3 * ROWS_Y - 1)
    widen(0)
    for load in loads:
        load.wait()
    ahead.start()
    for dy in range(1, ROWS_Y):
        @pl.when(y + dy < ROWS_Y)
        def _(dy=dy):
            sideways(dy).start()

    earlier = lax.broadcasted_iota(jnp.int32, (TOK, TOK), 0) < lax.broadcasted_iota(jnp.int32, (TOK, TOK), 1)
    later = lax.broadcasted_iota(jnp.int32, (TOK, TOK), 0) > lax.broadcasted_iota(jnp.int32, (TOK, TOK), 1)
    diagonal = ~(earlier | later)
    slot_cols = []
    for h in range(PAIR):
        id_row = id_ref[h]
        id_col = jnp.sum(jnp.where(diagonal, id_row, 0), axis=1, keepdims=True)
        same = id_col == id_row
        rank_row = jnp.sum(jnp.where(same & earlier, 1, 0), axis=0, keepdims=True)
        rank_col = jnp.sum(jnp.where(same & later, 1, 0), axis=1, keepdims=True)
        slot_row = id_row * SRC_CAP + rank_row
        slot_cols.append(id_col * SRC_CAP + rank_col)
        pick = jnp.where(lax.broadcasted_iota(jnp.int32, (SLOTS, TOK), 0) == slot_row, 1.0, 0.0)
        blank = (1.0 - jnp.sum(pick, axis=1, keepdims=True)) * EMPTY
        pick = pick.astype(jnp.bfloat16)
        cols = pl.ds(SPLIT + h * HD, HD)
        packed_q = dot(pick, q_ref[:, cols])
        packed_k = dot(pick, k_ref[:, cols])
        packed_v = dot(pick, v_ref[:, cols]) + blank
        for n, packed in enumerate((packed_q, packed_k, packed_v)):
            send[h, :, :, n * HD:(n + 1) * HD] = packed.reshape(SEQ, ROOM, HD).astype(jnp.bfloat16)

    def push(source, target, from_sem, to_sem):
        def act(peer):
            pltpu.make_async_remote_copy(
                src_ref=source.at[peer], dst_ref=target.at[me],
                send_sem=from_sem, recv_sem=to_sem, device_id={"seq": peer},
            ).start()
        return act

    def leg(h, dy):
        to_y = (y + dy) % ROWS_Y
        return pltpu.make_async_remote_copy(
            src_ref=send.at[h, (z + 8) % ROWS_Z * ROWS_Y + to_y], dst_ref=stop.at[h, y],
            send_sem=leg_send.at[h], recv_sem=leg_recv.at[h],
            device_id={"seq": (z + 12) % ROWS_Z * ROWS_Y + to_y},
        )

    def legs(h):
        return pltpu.make_async_remote_copy(
            src_ref=stop.at[h], dst_ref=stop.at[h], send_sem=leg_send.at[h], recv_sem=leg_recv.at[h],
            device_id={"seq": (me + 1) % SEQ},
        )

    def onward(h):
        return pltpu.make_async_remote_copy(
            src_ref=stop.at[h], dst_ref=recv.at[h, pl.ds((z + 4) % ROWS_Z * ROWS_Y, ROWS_Y)],
            send_sem=hop_send.at[h], recv_sem=recv_sem.at[h],
            device_id={"seq": (z + 12) % ROWS_Z * ROWS_Y + y},
        )

    def arrived(buffer, from_sem, to_sem):
        return pltpu.make_async_remote_copy(
            src_ref=buffer.at[pl.ds(0, SEQ - 1)], dst_ref=buffer.at[pl.ds(0, SEQ - 1)],
            send_sem=from_sem, recv_sem=to_sem, device_id={"seq": (me + 1) % SEQ},
        )

    def own_chunk(source, target, sem):
        return pltpu.make_async_copy(source.at[me], target.at[me], sem)

    first_push = push(send.at[0], recv.at[0], send_sem.at[0], recv_sem.at[0])
    for dz in (1, -1, 0):
        at_distance(dz, first_push, dz != 0)
    for n, distances in enumerate(((2,), (4, 3), (7, 6, 5))):
        pl.semaphore_wait(ready.at[n], 2)
        if n < 2:
            widen(n + 1)
        if n == 2:
            for dy in range(ROWS_Y):
                leg(0, dy).start()
        for d in distances:
            at_distance(d, first_push)
            at_distance(-d, first_push)
    for dy in range(ROWS_Y):
        leg(1, dy).start()
    legs(0).wait_recv()
    onward(0).start()
    each_peer(push(send.at[1], recv.at[1], send_sem.at[1], recv_sem.at[1]), 1)
    for h in range(PAIR):
        own_chunk(send.at[h], recv.at[h], own_sem.at[h]).start()

    legs(1).wait_recv()
    onward(1).start()
    ahead.wait_recv()
    for dy in range(1, ROWS_Y):
        @pl.when(y + dy >= ROWS_Y)
        def _(dy=dy):
            sideways(dy).start()

    def routed(h):
        arrived(recv.at[h], send_sem.at[h], recv_sem.at[h]).wait_recv()
        own_chunk(send.at[h], recv.at[h], own_sem.at[h]).wait()
        q, k, v = (
            recv[h, :, :, n * HD:(n + 1) * HD].astype(jnp.float32).reshape(SLOTS, HD).astype(jnp.bfloat16)
            for n in range(3)
        )
        probe = jnp.where(lax.broadcasted_iota(jnp.int32, (16, HD), 1) == 0, 1.0, 0.0).astype(jnp.bfloat16)
        first = dot(probe, v, NT)[0:1, :]
        absent = jnp.where(first > EMPTY_TEST, MASKED, 0.0)
        block = 128
        for b in range(SLOTS // block):
            lo, hi = b * block, (b + 1) * block
            row = lax.broadcasted_iota(jnp.int32, (block, hi), 0) + lo
            col = lax.broadcasted_iota(jnp.int32, (block, hi), 1)
            allowed = (col <= row) & ((row & (ROOM - SRC_CAP)) == (col & (ROOM - SRC_CAP)))
            scores = dot(q[lo:hi], k[:hi], NT) * scale + absent[:, :hi]
            mixed = blend(jnp.where(allowed, scores, MASKED), v[:hi])
            osend[h, b * 16:(b + 1) * 16] = mixed.reshape(16, ROOM, HD).astype(jnp.bfloat16)
        each_peer(push(osend.at[h], home.at[h], osend_sem.at[h], home_sem.at[h]))
        own_chunk(osend.at[h], home.at[h], own_sem.at[2 + h]).start()

    routed(0)
    routed(1)

    for dy in range(1, ROWS_Y):
        sideways(dy).wait_recv()
    width = (SPAN + 1) * TOK
    row = lax.broadcasted_iota(jnp.int32, (TOK, width), 0)
    col = lax.broadcasted_iota(jnp.int32, (TOK, width), 1)
    slot, at = col // TOK, col % TOK
    gap = row - at + slot * TOK
    allowed = (gap >= 0) & (gap < SPAN * TOK) & (slot <= me)
    for h in range(PAIR):
        k = win[:, :, h * HD:(h + 1) * HD].reshape(width, HD)
        v = win[:, :, SPLIT + h * HD:SPLIT + (h + 1) * HD].reshape(width, HD)
        scores = dot(q_ref[:, h * HD:(h + 1) * HD], k, NT) * scale
        mixed = blend(jnp.where(allowed, scores, MASKED), v)
        out_ref[:, h * HD:(h + 1) * HD] = mixed.astype(jnp.bfloat16)

    for h in range(PAIR):
        back = jnp.where(lax.broadcasted_iota(jnp.int32, (TOK, SLOTS), 1) == slot_cols[h], 1.0, 0.0).astype(jnp.bfloat16)
        arrived(home.at[h], osend_sem.at[h], home_sem.at[h]).wait_recv()
        own_chunk(osend.at[h], home.at[h], own_sem.at[2 + h]).wait()
        rows = home[h].astype(jnp.float32).reshape(SLOTS, HD).astype(jnp.bfloat16)
        out_ref[:, SPLIT + h * HD:SPLIT + (h + 1) * HD] = dot(back, rows).astype(jnp.bfloat16)

    for h in range(PAIR):
        sent = send.at[h, pl.ds(0, SEQ - 1 - ROWS_Y)]
        pltpu.make_async_remote_copy(
            src_ref=sent, dst_ref=sent, send_sem=send_sem.at[h], recv_sem=recv_sem.at[h],
            device_id={"seq": (me + 1) % SEQ},
        ).wait_send()
        legs(h).wait_send()
        onward(h).wait_send()
        arrived(home.at[h], osend_sem.at[h], home_sem.at[h]).wait_send()
    ahead.wait_send()
    for dy in range(1, ROWS_Y):
        sideways(dy).wait_send()


def per_device(query_rows, key_rows, value_rows, cluster_ids):
    vmem = pl.BlockSpec(memory_space=pltpu.VMEM)
    return pl.pallas_call(
        kernel,
        out_shape=jax.ShapeDtypeStruct(query_rows.shape, jnp.bfloat16),
        in_specs=[pl.BlockSpec(memory_space=pltpu.HBM)] * 4,
        out_specs=vmem,
        scratch_shapes=[
            pltpu.VMEM((TOK, 2 * SPLIT), jnp.bfloat16),
            pltpu.VMEM((TOK, 2 * SPLIT), jnp.bfloat16),
            pltpu.VMEM((TOK, 2 * SPLIT), jnp.bfloat16),
            pltpu.VMEM((PAIR, 1, TOK), jnp.int32),
            pltpu.VMEM((PAIR, SEQ, ROOM, 3 * HD), jnp.bfloat16),
            pltpu.VMEM((PAIR, SEQ, ROOM, 3 * HD), jnp.bfloat16),
            pltpu.VMEM((PAIR, SEQ, ROOM, HD), jnp.bfloat16),
            pltpu.VMEM((PAIR, SEQ, ROOM, HD), jnp.bfloat16),
            pltpu.VMEM((SPAN + 1, TOK, 2 * SPLIT), jnp.bfloat16),
            pltpu.VMEM((PAIR, ROWS_Y, ROOM, 3 * HD), jnp.bfloat16),
            pltpu.SemaphoreType.DMA((6,)),
            pltpu.SemaphoreType.DMA((4,)),
            pltpu.SemaphoreType.DMA((PAIR,)),
            pltpu.SemaphoreType.DMA((PAIR,)),
            pltpu.SemaphoreType.DMA((PAIR,)),
            pltpu.SemaphoreType.DMA((PAIR,)),
            pltpu.SemaphoreType.DMA((SPAN,)),
            pltpu.SemaphoreType.DMA((SPAN,)),
            pltpu.SemaphoreType.REGULAR((3,)),
            pltpu.SemaphoreType.DMA((PAIR,)),
            pltpu.SemaphoreType.DMA((PAIR,)),
            pltpu.SemaphoreType.DMA((PAIR,)),
        ],
        compiler_params=pltpu.CompilerParams(
            collective_id=0, has_side_effects=True, vmem_limit_bytes=67043328
        ),
    )(query_rows, key_rows, value_rows, cluster_ids.transpose(0, 2, 1))


def solution(mesh):
    in_specs = (P("seq", "head"), P("seq", "head"), P("seq", "head"), P("head", "seq", None))
    out_specs = P("seq", "head")
    return jax.shard_map(
        per_device, mesh=mesh, in_specs=in_specs, out_specs=out_specs, check_vma=False
    )
```

```python
import math

import jax
import jax.numpy as jnp
from jax import lax
from jax.experimental import pallas as pl
from jax.experimental.pallas import tpu as pltpu
from jax.sharding import PartitionSpec as P

CLUSTERS = 256
SRC_CAP = 2
SEQ = 64
ROWS_Z = 16
ROWS_Y = 4
TOK = 256
HD = 128
PAIR = 2
SPLIT = PAIR * HD
OWNED = CLUSTERS // SEQ
ROOM = OWNED * SRC_CAP
SLOTS = SEQ * ROOM
SPAN = 4
MASKED = -1e30
EMPTY = 2.0**60
EMPTY_TEST = 2.0**50
NT = (((1,), (1,)), ((), ()))


def dot(a, b, dims=(((1,), (0,)), ((), ()))):
    return lax.dot_general(a, b, dims, preferred_element_type=jnp.float32)


def blend(scores, value_block):
    largest = jnp.max(scores, axis=-1, keepdims=True)
    raised = jnp.exp(scores - largest)
    weights = (raised * (1.0 / jnp.sum(raised, axis=-1, keepdims=True))).astype(jnp.bfloat16)
    return dot(weights, value_block)


def kernel(q_hbm, k_hbm, v_hbm, id_hbm, out_ref,
           q_ref, k_ref, v_ref, id_ref, send, recv, osend, home, win, stop,
           load_sem, own_sem, send_sem, recv_sem, osend_sem, home_sem, win_send, win_recv, ready,
           leg_send, leg_recv, hop_send):
    me = lax.axis_index("seq")
    z, y = me // ROWS_Y, me % ROWS_Y
    scale = 1.0 / math.sqrt(HD)

    def at_distance(dz, act, away=True):
        for dy in range(ROWS_Y):
            if away or dy:
                act((z + dz + ROWS_Z) % ROWS_Z * ROWS_Y + (y + dy) % ROWS_Y)

    def each_peer(act, nearer=0):
        def step(i, carry):
            m = (i + 1) // 2
            at_distance((8 - m) * (2 * (i % 2) - 1), act)
            return carry

        lax.fori_loop(nearer, ROWS_Z - 1, step, 0)
        at_distance(0, act, False)

    barrier = pltpu.get_barrier_semaphore()

    def greet(peer):
        pl.semaphore_signal(barrier, inc=1, device_id={"seq": peer})

    for dz in (1, -1, 0):
        at_distance(dz, greet, dz != 0)

    def widen(n):
        for dz in (1 << n, -(1 << n)):
            peer = (z + dz + ROWS_Z) % ROWS_Z * ROWS_Y + y
            pl.semaphore_signal(ready.at[n], inc=1, device_id={"seq": peer})

    loads = [
        pltpu.make_async_copy(source, target, load_sem.at[n])
        for n, (source, target) in enumerate(
            ((id_hbm, id_ref), (q_hbm, q_ref), (k_hbm, k_ref), (v_hbm, v_ref),
             (k_hbm.at[:, pl.ds(0, SPLIT)], win.at[0, :, pl.ds(0, SPLIT)]),
             (v_hbm.at[:, pl.ds(0, SPLIT)], win.at[0, :, pl.ds(SPLIT, SPLIT)]))
        )
    ]
    for load in loads:
        load.start()

    def window(src_slot, dst_slot, peer):
        return pltpu.make_async_remote_copy(
            src_ref=win.at[src_slot], dst_ref=win.at[dst_slot],
            send_sem=win_send.at[dst_slot - 1], recv_sem=win_recv.at[dst_slot - 1],
            device_id={"seq": peer},
        )

    ahead = window(0, SPAN, (me + ROWS_Y) % SEQ)

    def sideways(dy):
        return window(SPAN * ((y + dy) // ROWS_Y), dy, z * ROWS_Y + (y + dy) % ROWS_Y)

    pl.semaphore_wait(barrier, 3 * ROWS_Y - 1)
    widen(0)
    for load in loads:
        load.wait()
    ahead.start()
    for dy in range(1, ROWS_Y):
        @pl.when(y + dy < ROWS_Y)
        def _(dy=dy):
            sideways(dy).start()

    earlier = lax.broadcasted_iota(jnp.int32, (TOK, TOK), 0) < lax.broadcasted_iota(jnp.int32, (TOK, TOK), 1)
    later = lax.broadcasted_iota(jnp.int32, (TOK, TOK), 0) > lax.broadcasted_iota(jnp.int32, (TOK, TOK), 1)
    diagonal = ~(earlier | later)
    slot_cols = []
    for h in range(PAIR):
        id_row = id_ref[h]
        id_col = jnp.sum(jnp.where(diagonal, id_row, 0), axis=1, keepdims=True)
        same = id_col == id_row
        rank_row = jnp.sum(jnp.where(same & earlier, 1, 0), axis=0, keepdims=True)
        rank_col = jnp.sum(jnp.where(same & later, 1, 0), axis=1, keepdims=True)
        slot_row = id_row * SRC_CAP + rank_row
        slot_cols.append(id_col * SRC_CAP + rank_col)
        pick = jnp.where(lax.broadcasted_iota(jnp.int32, (SLOTS, TOK), 0) == slot_row, 1.0, 0.0)
        blank = (1.0 - jnp.sum(pick, axis=1, keepdims=True)) * EMPTY
        pick = pick.astype(jnp.bfloat16)
        cols = pl.ds(SPLIT + h * HD, HD)
        packed_q = dot(pick, q_ref[:, cols])
        packed_k = dot(pick, k_ref[:, cols])
        packed_v = dot(pick, v_ref[:, cols]) + blank
        for n, packed in enumerate((packed_q, packed_k, packed_v)):
            send[h, :, :, n * HD:(n + 1) * HD] = packed.reshape(SEQ, ROOM, HD).astype(jnp.bfloat16)

    def push(source, target, from_sem, to_sem):
        def act(peer):
            pltpu.make_async_remote_copy(
                src_ref=source.at[peer], dst_ref=target.at[me],
                send_sem=from_sem, recv_sem=to_sem, device_id={"seq": peer},
            ).start()
        return act

    def leg(h, dy):
        to_y = (y + dy) % ROWS_Y
        return pltpu.make_async_remote_copy(
            src_ref=send.at[h, (z + 8) % ROWS_Z * ROWS_Y + to_y], dst_ref=stop.at[h, y],
            send_sem=leg_send.at[h], recv_sem=leg_recv.at[h],
            device_id={"seq": (z + 12) % ROWS_Z * ROWS_Y + to_y},
        )

    def legs(h):
        return pltpu.make_async_remote_copy(
            src_ref=stop.at[h], dst_ref=stop.at[h], send_sem=leg_send.at[h], recv_sem=leg_recv.at[h],
            device_id={"seq": (me + 1) % SEQ},
        )

    def onward(h):
        return pltpu.make_async_remote_copy(
            src_ref=stop.at[h], dst_ref=recv.at[h, pl.ds((z + 4) % ROWS_Z * ROWS_Y, ROWS_Y)],
            send_sem=hop_send.at[h], recv_sem=recv_sem.at[h],
            device_id={"seq": (z + 12) % ROWS_Z * ROWS_Y + y},
        )

    def arrived(buffer, from_sem, to_sem):
        return pltpu.make_async_remote_copy(
            src_ref=buffer.at[pl.ds(0, SEQ - 1)], dst_ref=buffer.at[pl.ds(0, SEQ - 1)],
            send_sem=from_sem, recv_sem=to_sem, device_id={"seq": (me + 1) % SEQ},
        )

    def own_chunk(source, target, sem):
        return pltpu.make_async_copy(source.at[me], target.at[me], sem)

    first_push = push(send.at[0], recv.at[0], send_sem.at[0], recv_sem.at[0])
    for dz in (1, -1, 0):
        at_distance(dz, first_push, dz != 0)
    for n, distances in enumerate(((2,), (4, 3), (7, 6, 5))):
        pl.semaphore_wait(ready.at[n], 2)
        if n < 2:
            widen(n + 1)
        if n == 2:
            for dy in range(ROWS_Y):
                leg(0, dy).start()
        for d in distances:
            at_distance(d, first_push)
            at_distance(-d, first_push)
    for dy in range(ROWS_Y):
        leg(1, dy).start()
    ahead.wait_recv()
    for dy in range(1, ROWS_Y):
        @pl.when(y + dy >= ROWS_Y)
        def _(dy=dy):
            sideways(dy).start()
    legs(0).wait_recv()
    onward(0).start()
    each_peer(push(send.at[1], recv.at[1], send_sem.at[1], recv_sem.at[1]), 1)
    for h in range(PAIR):
        own_chunk(send.at[h], recv.at[h], own_sem.at[h]).start()

    legs(1).wait_recv()
    onward(1).start()
    def routed(h):
        arrived(recv.at[h], send_sem.at[h], recv_sem.at[h]).wait_recv()
        own_chunk(send.at[h], recv.at[h], own_sem.at[h]).wait()
        q, k, v = (
            recv[h, :, :, n * HD:(n + 1) * HD].astype(jnp.float32).reshape(SLOTS, HD).astype(jnp.bfloat16)
            for n in range(3)
        )
        probe = jnp.where(lax.broadcasted_iota(jnp.int32, (16, HD), 1) == 0, 1.0, 0.0).astype(jnp.bfloat16)
        first = dot(probe, v, NT)[0:1, :]
        absent = jnp.where(first > EMPTY_TEST, MASKED, 0.0)
        block = 128
        for b in range(SLOTS // block):
            lo, hi = b * block, (b + 1) * block
            row = lax.broadcasted_iota(jnp.int32, (block, hi), 0) + lo
            col = lax.broadcasted_iota(jnp.int32, (block, hi), 1)
            allowed = (col <= row) & ((row & (ROOM - SRC_CAP)) == (col & (ROOM - SRC_CAP)))
            scores = dot(q[lo:hi], k[:hi], NT) * scale + absent[:, :hi]
            mixed = blend(jnp.where(allowed, scores, MASKED), v[:hi])
            osend[h, b * 16:(b + 1) * 16] = mixed.reshape(16, ROOM, HD).astype(jnp.bfloat16)
        each_peer(push(osend.at[h], home.at[h], osend_sem.at[h], home_sem.at[h]))
        own_chunk(osend.at[h], home.at[h], own_sem.at[2 + h]).start()

    routed(0)
    for dy in range(1, ROWS_Y):
        sideways(dy).wait_recv()
    width = (SPAN + 1) * TOK
    row = lax.broadcasted_iota(jnp.int32, (TOK, width), 0)
    col = lax.broadcasted_iota(jnp.int32, (TOK, width), 1)
    slot, at = col // TOK, col % TOK
    gap = row - at + slot * TOK
    allowed = (gap >= 0) & (gap < SPAN * TOK) & (slot <= me)
    for h in range(PAIR):
        k = win[:, :, h * HD:(h + 1) * HD].reshape(width, HD)
        v = win[:, :, SPLIT + h * HD:SPLIT + (h + 1) * HD].reshape(width, HD)
        scores = dot(q_ref[:, h * HD:(h + 1) * HD], k, NT) * scale
        mixed = blend(jnp.where(allowed, scores, MASKED), v)
        out_ref[:, h * HD:(h + 1) * HD] = mixed.astype(jnp.bfloat16)

    routed(1)

    for h in range(PAIR):
        back = jnp.where(lax.broadcasted_iota(jnp.int32, (TOK, SLOTS), 1) == slot_cols[h], 1.0, 0.0).astype(jnp.bfloat16)
        arrived(home.at[h], osend_sem.at[h], home_sem.at[h]).wait_recv()
        own_chunk(osend.at[h], home.at[h], own_sem.at[2 + h]).wait()
        rows = home[h].astype(jnp.float32).reshape(SLOTS, HD).astype(jnp.bfloat16)
        out_ref[:, SPLIT + h * HD:SPLIT + (h + 1) * HD] = dot(back, rows).astype(jnp.bfloat16)

    for h in range(PAIR):
        sent = send.at[h, pl.ds(0, SEQ - 1 - ROWS_Y)]
        pltpu.make_async_remote_copy(
            src_ref=sent, dst_ref=sent, send_sem=send_sem.at[h], recv_sem=recv_sem.at[h],
            device_id={"seq": (me + 1) % SEQ},
        ).wait_send()
        legs(h).wait_send()
        onward(h).wait_send()
        arrived(home.at[h], osend_sem.at[h], home_sem.at[h]).wait_send()
    ahead.wait_send()
    for dy in range(1, ROWS_Y):
        sideways(dy).wait_send()


def per_device(query_rows, key_rows, value_rows, cluster_ids):
    vmem = pl.BlockSpec(memory_space=pltpu.VMEM)
    return pl.pallas_call(
        kernel,
        out_shape=jax.ShapeDtypeStruct(query_rows.shape, jnp.bfloat16),
        in_specs=[pl.BlockSpec(memory_space=pltpu.HBM)] * 4,
        out_specs=vmem,
        scratch_shapes=[
            pltpu.VMEM((TOK, 2 * SPLIT), jnp.bfloat16),
            pltpu.VMEM((TOK, 2 * SPLIT), jnp.bfloat16),
            pltpu.VMEM((TOK, 2 * SPLIT), jnp.bfloat16),
            pltpu.VMEM((PAIR, 1, TOK), jnp.int32),
            pltpu.VMEM((PAIR, SEQ, ROOM, 3 * HD), jnp.bfloat16),
            pltpu.VMEM((PAIR, SEQ, ROOM, 3 * HD), jnp.bfloat16),
            pltpu.VMEM((PAIR, SEQ, ROOM, HD), jnp.bfloat16),
            pltpu.VMEM((PAIR, SEQ, ROOM, HD), jnp.bfloat16),
            pltpu.VMEM((SPAN + 1, TOK, 2 * SPLIT), jnp.bfloat16),
            pltpu.VMEM((PAIR, ROWS_Y, ROOM, 3 * HD), jnp.bfloat16),
            pltpu.SemaphoreType.DMA((6,)),
            pltpu.SemaphoreType.DMA((4,)),
            pltpu.SemaphoreType.DMA((PAIR,)),
            pltpu.SemaphoreType.DMA((PAIR,)),
            pltpu.SemaphoreType.DMA((PAIR,)),
            pltpu.SemaphoreType.DMA((PAIR,)),
            pltpu.SemaphoreType.DMA((SPAN,)),
            pltpu.SemaphoreType.DMA((SPAN,)),
            pltpu.SemaphoreType.REGULAR((3,)),
            pltpu.SemaphoreType.DMA((PAIR,)),
            pltpu.SemaphoreType.DMA((PAIR,)),
            pltpu.SemaphoreType.DMA((PAIR,)),
        ],
        compiler_params=pltpu.CompilerParams(
            collective_id=0, has_side_effects=True, vmem_limit_bytes=67043328
        ),
    )(query_rows, key_rows, value_rows, cluster_ids.transpose(0, 2, 1))


def solution(mesh):
    in_specs = (P("seq", "head"), P("seq", "head"), P("seq", "head"), P("head", "seq", None))
    out_specs = P("seq", "head")
    return jax.shard_map(
        per_device, mesh=mesh, in_specs=in_specs, out_specs=out_specs, check_vma=False
    )
```
